128 devices in a mesh: dev: 32 (over z, x, core), rep: 4 (over y).
Axes of the slice: x: 4, y: 4, z: 4, core: 2. Of those that a mesh axis runs over, the one named last changes fastest.
Arguments:
- activations: bfloat16 [4, 256, 64, 2048], P('rep', 'dev'), may hold values from -6 to 6
- out_grads: bfloat16 [4, 256, 64, 1024], P('rep', 'dev'), may hold values from -6 to 6
- inverse: float32 [32, 2048, 2048], P('dev'), may hold values from -4 to 11, as said below
Outputs:
- whitened: float32 [4, 256, 65536], P('rep', 'dev')
- leverage: float32 [4, 256], P('rep', 'dev')
- new_inverse: float32 [32, 2048, 2048], P('dev', 'rep')
The draws below stay inside these ranges and needn't reach their ends.
Inputs may be any that keep to these rules, and one draw needn't show every extreme that they name: Each 2048 x 2048 matrix of inverse is symmetric positive definite.
All inputs are finite; a program needn't handle non-finite values.
Results may differ from the reference program's by a relative error of at most 0.0003.
Values sent between devices are 32-bit elements; how exact they have to be, the bound alone decides.
No kernel may reach another device: no remote copies, remote signals or barrier semaphores. Data moves between devices by JAX's collectives and lax.ppermute only.
A program may use at most 128 MiB of HBM per device.

```python
import jax
import jax.numpy as jnp
from jax import lax

KI = 64
KO = 32
KF = 2048
TOK = 64
MODS = 32
GROUP = 256
GROUPS = 4


def draw_inverse(key, part):
    first_key, second_key = jax.random.split(jax.random.fold_in(key, 17))
    growth = jnp.exp(jnp.log(3.0) * jnp.arange(MODS, dtype=jnp.float32) / max(MODS - 1, 1))
    factor = jax.random.uniform(second_key, (MODS,), jnp.float32, 1.0, 1.5)
    unit = jnp.clip(jax.random.normal(first_key, (MODS, KF, KF), jnp.float32), -5.0, 5.0)
    gaussian = unit * (0.35 / KF ** 0.5)
    symmetric = (gaussian + jnp.swapaxes(gaussian, 1, 2)) / 2.0 ** 0.5
    module_scale = growth * factor
    return (module_scale[:, None, None] * (jnp.eye(KF, dtype=jnp.float32)[None] + symmetric)).astype(jnp.float32)


def steps_of(own_key, dims, cuts, low, top_value):
    gain = 1.0
    for axis_at, parts in cuts:
        steps = jax.random.uniform(jax.random.fold_in(jax.random.fold_in(own_key, 6), axis_at), (parts,), jnp.float32, low / len(cuts), top_value / len(cuts))
        gain = gain * jnp.repeat(jnp.exp(steps), dims[axis_at] // parts).reshape((-1,) + (1,) * (len(dims) - 1 - axis_at))
    return gain


def scatter_about(rng, dims, spread, most, cuts=(), kind=jnp.bfloat16):
    loudness = steps_of(rng, dims, cuts, -0.22, 0.18) if cuts else 1.0
    values = jax.random.normal(rng, dims, jnp.float32) * spread * loudness
    return jnp.minimum(jnp.maximum(values, -most), most).astype(kind)


def setup_inputs(seed: int = 0) -> dict:
    streams_of = jax.random.split(jax.random.key(seed), 4)
    activations = scatter_about(streams_of[0], (GROUPS, GROUP, TOK, MODS * KI), 1.0, 6.0, ((0, 4), (1, 32)))
    out_grads = scatter_about(streams_of[1], (GROUPS, GROUP, TOK, MODS * KO), 1.0, 6.0, ((0, 4), (1, 32)))
    inverse = draw_inverse(jax.random.fold_in(streams_of[3], 71), 0)
    return {"activations": activations, "out_grads": out_grads, "inverse": inverse}


def reference(activations, out_grads, inverse):
    total = GROUPS * GROUP
    acts_f = activations.reshape(total, TOK, MODS, KI).astype(jnp.float32)
    grads_f = out_grads.reshape(total, TOK, MODS, KO).astype(jnp.float32)
    features = jnp.einsum('ntmo,ntmi->mnoi', grads_f, acts_f, precision=lax.Precision.HIGHEST)
    features = features.reshape(MODS, total, KF) * TOK ** (-0.5)
    white = jnp.einsum('mnk,mkl->mnl', features, inverse, precision=lax.Precision.HIGHEST)
    leverage = jnp.sum(features * white, axis=(0, 2)) / (MODS * KF)
    damping = 1.0 + KF * leverage

    def update(packed):
        rows_m, white_m, inverse_m = packed
        capacitance = jnp.dot(rows_m, white_m.T, precision=lax.Precision.HIGHEST) + jnp.diag(damping)
        factor = jnp.linalg.cholesky(capacitance)
        solved = jax.scipy.linalg.cho_solve((factor, True), white_m)
        return inverse_m - jnp.dot(white_m.T, solved, precision=lax.Precision.HIGHEST)
    new_inverse = lax.map(update, (features, white, inverse))
    whitened = white.transpose(1, 0, 2).reshape(GROUPS, GROUP, MODS * KF)
    return (whitened, leverage.reshape(GROUPS, GROUP), new_inverse)
```

```python
import jax
import jax.numpy as jnp
from jax import lax
from jax.experimental import pallas as pl
from jax.experimental.pallas import tpu as pltpu
from jax.sharding import PartitionSpec as P

KI = 64
KO = 32
BLK = 128
NT = (((1,), (1,)), ((), ()))
NN = (((1,), (0,)), ((), ()))
F32 = jnp.float32
BF16 = jnp.bfloat16


def split(x):
    hi = x.astype(BF16)
    return hi, (x - hi.astype(F32)).astype(BF16)


def dot3(a, b, dims):
    one = lambda x, y: lax.dot_general(x, y, dims, preferred_element_type=F32)
    return one(a[0], b[0]) + (one(a[0], b[1]) + one(a[1], b[0]))


def lane_bcast(v, index):
    return jnp.take_along_axis(v, jnp.full((8, 128), index, jnp.int32), axis=1)


def sweep_pair(rows, base, jj, lane, sub):
    top = rows[0]
    r0 = jnp.broadcast_to(top[jj : jj + 1, :], (8, 128))
    r1 = jnp.broadcast_to(top[jj + 1 : jj + 2, :], (8, 128))
    at0 = lane == base + jj
    at1 = lane == base + jj + 1
    p00, p01, p11 = lane_bcast(r0, base + jj), lane_bcast(r0, base + jj + 1), lane_bcast(r1, base + jj + 1)
    inv_det = 1.0 / (p00 * p11 - p01 * p01)
    q00, q01, q11 = p11 * inv_det, -p01 * inv_det, p00 * inv_det
    n0 = q00 * r0 + q01 * r1
    n1 = q01 * r0 + q11 * r1
    n0 = jnp.where(at0, -q00, jnp.where(at1, -q01, n0))
    n1 = jnp.where(at0, -q01, jnp.where(at1, -q11, n1))
    out = []
    for i, a in enumerate(rows):
        v = jnp.where(at0 | at1, 0.0, a) - lane_bcast(a, base + jj) * n0 - lane_bcast(a, base + jj + 1) * n1
        if i == 0:
            v = jnp.where(sub == jj, n0, jnp.where(sub == jj + 1, n1, v))
        out.append(v)
    return out


def spd_inverse(s):
    lane = lax.broadcasted_iota(jnp.int32, (8, 128), 1)
    sub = lax.broadcasted_iota(jnp.int32, (8, 128), 0)
    count = BLK // 8

    def step(c, rows):
        rows = list(rows)
        for jj in range(0, 8, 2):
            rows = sweep_pair(rows, c * 8, jj, lane, sub)
        return tuple(rows[1:] + rows[:1])

    rows = lax.fori_loop(0, count, step, tuple(s[8 * i : 8 * i + 8, :] for i in range(count)))
    return -jnp.concatenate(rows, axis=0)


def group_kernel(prev):
    def kernel(*refs):
        f_ref, w_ref, d_ref = refs[:3]
        state = refs[3 : 3 + 4 * prev]
        zh_ref, zl_ref, xh_ref, xl_ref = refs[3 + 4 * prev :]
        f = split(f_ref[...])
        z = w_ref[...]
        for p in range(prev):
            zh, zl, xh, xl = state[4 * p : 4 * p + 4]
            coef = split(dot3(f, (xh[...], xl[...]), NT))
            z = z - dot3(coef, (zh[...], zl[...]), NN)
        zs = split(z)
        s = dot3(f, zs, NT)
        n = s.shape[0]
        eye = lax.broadcasted_iota(jnp.int32, (n, n), 0) == lax.broadcasted_iota(jnp.int32, (n, n), 1)
        s = s + jnp.where(eye, jnp.broadcast_to(d_ref[...], (n, n)), 0.0)
        z0h, z0l = zs[0][:BLK], zs[1][:BLK]
        inv0 = split(spd_inverse(s[:BLK, :BLK]))
        x0 = split(dot3(inv0, (z0h, z0l), NN))
        s10 = split(s[BLK:, :BLK])
        t = split(dot3(s10, inv0, NN))
        z1 = split(z[BLK:] - dot3(t, (z0h, z0l), NN))
        inv1 = split(spd_inverse(s[BLK:, BLK:] - dot3(t, s10, NT)))
        x1 = split(dot3(inv1, z1, NN))
        zh_ref[:BLK], zl_ref[:BLK] = z0h, z0l
        xh_ref[:BLK], xl_ref[:BLK] = x0
        zh_ref[BLK:], zl_ref[BLK:] = z1
        xh_ref[BLK:], xl_ref[BLK:] = x1

    return kernel


def group_step(f, w, damping, state):
    prev = len(state)
    out = jax.ShapeDtypeStruct(f.shape, BF16)
    return pl.pallas_call(
        group_kernel(prev),
        out_shape=(out, out, out, out),
        name=f"group{prev}",
        compiler_params=pltpu.CompilerParams(vmem_limit_bytes=48 << 20),
    )(f, w, damping, *[a for s in state for a in s])


def body(activations, out_grads, inverse):
    num_dev = lax.axis_size("dev")
    num_rep = lax.axis_size("rep")
    examples = activations.shape[1]
    tokens = activations.shape[2]
    width = KI * KO
    group_rows = examples * num_dev
    acts_four = activations.reshape(examples, tokens, num_dev, KI)
    grads_four = out_grads.reshape(examples, tokens, num_dev, KO)
    features = jnp.einsum("etmo,etmi->emoi", grads_four, acts_four, preferred_element_type=F32)
    features = features.reshape(examples, num_dev, width) * tokens ** (-0.5)
    own = lax.all_to_all(features, "dev", split_axis=1, concat_axis=0, tiled=True)[:, 0, :]
    v = inverse[0]
    white_of = lambda rows: jnp.dot(rows, v, precision=lax.Precision.HIGH)

    up = [(i, (i + 1) % num_rep) for i in range(num_rep)]
    down = [(i, (i - 1) % num_rep) for i in range(num_rep)]
    across = [(i, (i + 2) % num_rep) for i in range(num_rep)]
    half = group_rows // 2
    below = lax.ppermute(own, "rep", up)
    above = lax.ppermute(own, "rep", down)
    far = jnp.concatenate(
        [lax.ppermute(below[:half], "rep", up), lax.ppermute(above[half:], "rep", down)], axis=0
    )

    white = white_of(own)
    terms = jnp.sum(own * white, axis=1)
    spread = lax.all_to_all(
        jnp.broadcast_to(terms[None], (num_dev, group_rows)), "dev", split_axis=0, concat_axis=0, tiled=True
    )
    lev = jnp.sum(spread, axis=0) / (num_dev * width)
    damp = lambda a: (1.0 + width * a)[None]
    lev_below, lev_above, lev_far = (lax.ppermute(lev, "rep", p) for p in (up, down, across))

    state = [group_step(own, white, damp(lev), [])]
    for rows, level in ((below, lev_below), (above, lev_above), (far, lev_far)):
        state.append(group_step(rows, white_of(rows), damp(level), state))

    count = width // num_rep
    first = lax.axis_index("rep") * count
    zh, zl, xh, xl = (jnp.concatenate([s[i] for s in state], axis=0) for i in range(4))
    cut = lambda a: lax.dynamic_slice_in_dim(a, first, count, 1)
    tn = lambda a, b: lax.dot_general(a, b, (((0,), (0,)), ((), ())), preferred_element_type=F32)
    change = tn(cut(zh), xh) + tn(cut(zh), xl) + tn(cut(zl), xh)
    updated = lax.dynamic_slice_in_dim(v, first, count, 0) - change

    returned = lax.all_to_all(
        white.reshape(num_dev, examples, 1, width), "dev", split_axis=0, concat_axis=2, tiled=True
    )
    whitened_out = returned.reshape(1, examples, num_dev * width)
    lev_out = lax.dynamic_slice_in_dim(lev, lax.axis_index("dev") * examples, examples, 0)[None]
    return (whitened_out, lev_out, updated.reshape(1, count, width))


def solution(mesh):
    in_specs = (P("rep", "dev", None, None), P("rep", "dev", None, None), P("dev", None, None))
    out_specs = (P("rep", "dev", None), P("rep", "dev"), P("dev", "rep", None))
    return jax.shard_map(body, mesh=mesh, in_specs=in_specs, out_specs=out_specs, check_vma=False)
```

```python
import jax
import jax.numpy as jnp
from jax import lax
from jax.experimental import pallas as pl
from jax.experimental.pallas import tpu as pltpu
from jax.sharding import PartitionSpec as P

KI = 64
KO = 32
BLK = 128
TILE = 256
NT = (((1,), (1,)), ((), ()))
NN = (((1,), (0,)), ((), ()))
F32 = jnp.float32
BF16 = jnp.bfloat16
ANY = pl.BlockSpec(memory_space=pltpu.HBM)
VMEM = pl.BlockSpec(memory_space=pltpu.VMEM)


def split(x):
    hi = x.astype(BF16)
    return hi, (x - hi.astype(F32)).astype(BF16)


def dot3(a, b, dims):
    (ka,), (kb,) = dims[0]
    a = jnp.concatenate([a[0], a[0], a[1]], axis=ka)
    b = jnp.concatenate([b[0], b[1], b[0]], axis=kb)
    return lax.dot_general(a, b, dims, preferred_element_type=F32)


def get(ref, rows=slice(None), first=0, count=None):
    count = ref.shape[0] if count is None else count
    return jnp.concatenate([ref[first + i, rows, :] for i in range(count)], axis=1)


def put(refs, pair, rows=slice(None)):
    for ref, x in zip(refs, pair):
        for i in range(ref.shape[0]):
            ref[i, rows, :] = x[:, i * 128 : (i + 1) * 128]


def lane_bcast(v, index):
    return jnp.take_along_axis(v, jnp.full((8, 128), index, jnp.int32), axis=1)


def sweep_pair(rows, head, base, jj, lane, sub, side):
    top = rows[head]
    r0 = jnp.broadcast_to(top[jj : jj + 1, :], (8, 128))
    r1 = jnp.broadcast_to(top[jj + 1 : jj + 2, :], (8, 128))
    at0 = lane == base + jj
    at1 = lane == base + jj + 1
    p00, p01, p11 = lane_bcast(r0, base + jj), lane_bcast(r0, base + jj + 1), lane_bcast(r1, base + jj + 1)
    side()
    inv_det = 1.0 / (p00 * p11 - p01 * p01)
    q00, q01, q11 = p11 * inv_det, -p01 * inv_det, p00 * inv_det
    n0 = q00 * r0 + q01 * r1
    n1 = q01 * r0 + q11 * r1
    n0 = jnp.where(at0, -q00, jnp.where(at1, -q01, n0))
    n1 = jnp.where(at0, -q01, jnp.where(at1, -q11, n1))
    out = []
    for i, a in enumerate(rows):
        v = jnp.where(at0 | at1, 0.0, a) - lane_bcast(a, base + jj) * n0 - lane_bcast(a, base + jj + 1) * n1
        if i == head:
            v = jnp.where(sub == jj, n0, jnp.where(sub == jj + 1, n1, v))
        out.append(v)
    return out


def spd_inverse(s, side=None):
    lane = lax.broadcasted_iota(jnp.int32, (8, 128), 1)
    sub = lax.broadcasted_iota(jnp.int32, (8, 128), 0)
    count = BLK // 8

    def step(c, rows):
        rows = list(rows)
        pieces = side(c)
        for q in range(4):
            for jj in range(0, 8, 2):
                rows = sweep_pair(rows, q, c * 32 + q * 8, jj, lane, sub, lambda: pieces(q * 4 + jj // 2))
        return tuple(rows[4:] + rows[:4])

    rows = lax.fori_loop(0, count // 4, step, tuple(s[8 * i : 8 * i + 8, :] for i in range(count)))
    return -jnp.concatenate(rows, axis=0)


def features_kernel(examples, tokens, pairs):
    def kernel(g_ref, a_ref, o_ref):
        n_out, depth = 2 * KO, g_ref.shape[1]
        own = lax.broadcasted_iota(jnp.int32, (1, examples, depth), 1) == (
            lax.broadcasted_iota(jnp.int32, (1, examples, depth), 2) // tokens
        )
        low = lax.broadcasted_iota(jnp.int32, (examples, 2 * KI), 1) < KI


        @pl.loop(0, pairs)
        def _(q):
            g = g_ref[pl.ds(pl.multiple_of(q * n_out, n_out), n_out), :].astype(F32)
            g = jnp.where(own, jnp.broadcast_to(g[:, None, :], (n_out, examples, depth)), 0.0)
            g = g.reshape(n_out * examples, depth).astype(BF16)
            acts = a_ref[:, pl.ds(pl.multiple_of(q * 2 * KI, 2 * KI), 2 * KI)]
            prod = lax.dot_general(g, acts, NN, preferred_element_type=F32) * tokens ** (-0.5)
            turned = pltpu.roll(prod, KI, 1)
            for m in range(2):
                left, right = (prod, turned) if m == 0 else (turned, prod)
                for t in range(KO // 2):
                    even = (m * KO + 2 * t) * examples
                    odd = even + examples
                    o_ref[2 * q + m, :, t * 128 : (t + 1) * 128] = jnp.where(
                        low, left[even : even + examples], right[odd : odd + examples]
                    )

    return kernel


def make_features(activations, out_grads, num_dev):
    _, examples, tokens, _ = activations.shape
    depth = examples * tokens
    pairs = num_dev // 8
    acts = activations.reshape(depth, num_dev * KI)
    grads = out_grads.reshape(depth, num_dev * KO).T
    return pl.pallas_call(
        features_kernel(examples, tokens, pairs),
        out_shape=jax.ShapeDtypeStruct((num_dev, examples, KI * KO), F32),
        grid=(num_dev // 2 // pairs,),
        in_specs=[
            pl.BlockSpec((pairs * 2 * KO, depth), lambda i: (i, 0)),
            pl.BlockSpec((depth, pairs * 2 * KI), lambda i: (0, i)),
        ],
        out_specs=pl.BlockSpec((2 * pairs, examples, KI * KO), lambda i: (i, 0, 0)),
        name="features",
    )(grads, acts)


def white_kernel(f_ref, v_ref, w_ref, vh_ref, vl_ref, t_ref, fh, fl, acc):
    n = pl.program_id(0)

    @pl.when(n == 0)
    def _():
        fh[...], fl[...] = split(f_ref[...])
        acc[...] = jnp.zeros_like(acc)

    vh, vl = split(v_ref[...])
    put((vh_ref, vl_ref), (vh, vl))
    w = dot3((fh[...], fl[...]), (vh, vl), NN)
    w_ref[...] = w
    part = w * f_ref[:, pl.ds(pl.multiple_of(n * TILE, TILE), TILE)]
    acc[...] += part[:, :128] + part[:, 128:]

    @pl.when(n == pl.num_programs(0) - 1)
    def _():
        ones = jnp.ones((t_ref.shape[0], 128), BF16)
        one = lambda x: lax.dot_general(ones, x, NT, preferred_element_type=F32)
        hi, _ = split(acc[...])
        mid, low = split(acc[...] - hi.astype(F32))
        t_ref[...] = one(hi) + (one(mid) + one(low))


def own_white(f, v, copies):
    rows, width = f.shape
    col = lambda n: (0, n)
    return pl.pallas_call(
        white_kernel,
        out_shape=(
            jax.ShapeDtypeStruct((rows, width), F32),
            jax.ShapeDtypeStruct((width // 128, width, 128), BF16),
            jax.ShapeDtypeStruct((width // 128, width, 128), BF16),
            jax.ShapeDtypeStruct((copies, rows), F32),
        ),
        grid=(width // TILE,),
        in_specs=[pl.BlockSpec((rows, width), lambda n: (0, 0)), pl.BlockSpec((width, TILE), col)],
        out_specs=(
            pl.BlockSpec((rows, TILE), col),
            pl.BlockSpec((TILE // 128, width, 128), lambda n: (n, 0, 0)),
            pl.BlockSpec((TILE // 128, width, 128), lambda n: (n, 0, 0)),
            pl.BlockSpec((copies, rows), lambda n: (0, 0)),
        ),
        scratch_shapes=[pltpu.VMEM((rows, width), BF16)] * 2 + [pltpu.VMEM((rows, 128), F32)],
        compiler_params=pltpu.CompilerParams(vmem_limit_bytes=58 << 20),
        name="own_white",
    )(f, v)


def group_step(parts, white, levels, state, following, start, v_pair, base, cost):
    last = not following
    prev = len(state)
    rows, width = white.shape
    steps = BLK // 8
    cols = width // 4
    n_tiles = width // TILE
    n_parts, n_lev, n_next = len(parts), len(levels), len(following)
    n_state = 6 * prev
    part_rows = rows // n_parts
    depth = width // 4

    def kernel(*refs):
        refs = list(refs)
        take = lambda k: [refs.pop(0) for _ in range(k)]
        (start_ref,) = take(1)
        f_in, (w_in,), lev_in, state_in, next_in = take(n_parts), take(1), take(n_lev), take(n_state), take(n_next)
        v_in = take(2) if not last else []
        (base_in,) = take(1) if last else (None,)
        outs = take(1) if last else take(6)
        (wn_out,) = take(1) if not last else (None,)
        f_buf, z_buf, d_buf, fh, fl, zh, zl, xh, xl, zth, ztl = take(11)
        stacks = take(6) if prev else []
        if last:
            (out_buf,) = take(1)
        else:
            fn_buf, fnh, fnl, vh, vl, wn_buf = take(6)
        in_sem, state_sem, side_sem, out_sem = take(4)
        copy = pltpu.make_async_copy

        def gather(srcs, dst, sem, at):
            size = rows // len(srcs)
            return [
                copy(x.at[pl.ds(0, size)], dst.at[pl.ds(i * size, size)], sem.at[at + i]) for i, x in enumerate(srcs)
            ]

        first_row = pl.multiple_of(start_ref[0], cols)
        f_copy = gather(f_in, f_buf, in_sem, 0)
        w_copy = gather([w_in], z_buf, in_sem, n_parts)
        lane, d_copy = 0, []
        for i, (ref, (_, at, size)) in enumerate(zip(lev_in, levels)):
            src = ref.at[pl.ds(ref.shape[0] - 8, 8), pl.ds(at, size)]
            d_copy.append(copy(src, d_buf.at[:, pl.ds(lane, size)], in_sem.at[n_parts + 1 + i]))
            lane += size
        s_copy = [copy(a, stacks[i % 6].at[i // 6], state_sem.at[i]) for i, a in enumerate(state_in)]
        for c in f_copy:
            c.start()
        for p in range(prev):
            for i in (2, 3):
                s_copy[6 * p + i].start()
            if p == 0:
                for c in w_copy + d_copy:
                    c.start()
            for i in (0, 1):
                s_copy[6 * p + i].start()
        if prev == 0:
            for c in w_copy + d_copy:
                c.start()
        if last:
            side_copy = [copy(base_in.at[pl.ds(first_row, cols)], out_buf, side_sem.at[0])]
            for p in range(prev):
                side_copy += s_copy[6 * p + 4 : 6 * p + 6]
        else:
            side_copy = gather(next_in, fn_buf, side_sem, 0)
            v_copy = lambda i, n: copy(
                v_in[i].at[pl.ds(2 * n, 2)], (vh, vl)[i].at[pl.ds(2 * n, 2)], side_sem.at[n_next + 2 * n + i]
            )
        for c in side_copy:
            c.start()
        if not last:
            for n in range(n_tiles):
                for i in range(2):
                    v_copy(i, n).start()
        for c in f_copy:
            c.wait()
        f = split(f_buf[...])
        put((fh, fl), f)
        for c in w_copy:
            c.wait()
        if prev:
            arrived = lambda p, i: copy(state_in[i], stacks[i].at[p], state_sem.at[6 * p + i]).wait()

            @pl.loop(0, prev)
            def _(p):
                ph, pl_, qh, ql = (stacks[i].at[p] for i in range(4))
                arrived(p, 2)
                arrived(p, 3)
                coef = split(dot3((get(fh), get(fl)), (get(qh), get(ql)), NT))
                arrived(p, 0)
                arrived(p, 1)
                z_buf[...] -= dot3(coef, (get(ph), get(pl_)), NN)

        put((zh, zl), split(z_buf[...]))
        s = dot3((get(fh), get(fl)), (get(zh), get(zl)), NT)
        for c in d_copy:
            c.wait()
        eye = lax.broadcasted_iota(jnp.int32, (rows, rows), 0) == lax.broadcasted_iota(jnp.int32, (rows, rows), 1)
        damping = 1.0 + width * d_buf[0:1, :]
        s = s + jnp.where(eye, jnp.broadcast_to(damping, (rows, rows)), 0.0)
        for c in side_copy:
            c.wait()
        if not last:
            put((fnh, fnl), split(fn_buf[...]))

        def side(block):
            if not last:

                def work(c):
                    n = block * 4 + c
                    v_copy(0, n).wait()
                    v_copy(1, n).wait()
                    total = []

                    def piece(i):
                        if i % 2:
                            return
                        k = slice(i * 128, (i + 2) * 128)
                        f_pair = (get(fnh, first=i, count=2), get(fnl, first=i, count=2))
                        one = dot3(f_pair, (get(vh, k, 2 * n, 2), get(vl, k, 2 * n, 2)), NN)
                        total[:] = [total[0] + one if total else one]
                        if i == 14:
                            wn_buf[:, pl.ds(pl.multiple_of(n * TILE, TILE), TILE)] = total[0]

                    return piece

                return work

            def work(c):
                def piece(i):
                    if i % 4:
                        return
                    n = 2 * c + i // 8
                    at = pl.multiple_of(n * TILE, TILE)
                    part = cols // 2
                    some = slice((i // 4) % 2 * part, ((i // 4) % 2 + 1) * part)
                    total = None
                    for p in range(2) if block == 0 else range(2, prev):
                        qh, ql, th, tl = (stacks[i].at[p] for i in range(2, 6))
                        a = (get(th, some), get(tl, some))
                        one = dot3(a, (get(qh, slice(None), 2 * n, 2), get(ql, slice(None), 2 * n, 2)), NN)
                        total = one if total is None else total + one
                    out_buf[some, pl.ds(at, TILE)] -= total

                return piece

            return work

        top, low = slice(0, BLK), slice(BLK, rows)
        inv0 = split(spd_inverse(s[:BLK, :BLK], side(0)))
        z0 = (get(zh, top), get(zl, top))
        put((xh, xl), split(dot3(inv0, z0, NN)), top)
        s10 = split(s[BLK:, :BLK])
        t = split(dot3(s10, inv0, NN))
        z_buf[BLK:] -= dot3(t, z0, NN)
        z1 = split(z_buf[BLK:])
        put((zh, zl), z1, low)
        s11 = s[BLK:, BLK:] - dot3(t, s10, NT)
        put((zth, ztl), split(z_buf[:, pl.ds(first_row, cols)].T))
        flush = []
        inv1 = split(spd_inverse(s11, side(1)))
        put((xh, xl), split(dot3(inv1, (get(zh, low), get(zl, low)), NN)), low)
        if last:
            for n in range(n_tiles):
                at = slice(n * TILE, (n + 1) * TILE)
                b = (get(xh, slice(None), 2 * n, 2), get(xl, slice(None), 2 * n, 2))
                out_buf[:, at] -= dot3((get(zth), get(ztl)), b, NN)
                flush.append(copy(out_buf.at[:, pl.ds(n * TILE, TILE)], outs[0].at[:, pl.ds(n * TILE, TILE)], out_sem.at[n]))
                flush[-1].start()
        else:
            flush = [copy(a, b, out_sem.at[i]) for i, (a, b) in enumerate(zip((zh, zl, xh, xl, zth, ztl), outs))]
            flush.append(copy(wn_buf, wn_out, out_sem.at[6]))
            for c in flush:
                c.start()
        for c in flush:
            c.wait()

    like = jax.ShapeDtypeStruct
    wide, cut = (width // 128, rows, 128), (rows // 128, cols, 128)
    if last:
        out_shape = [like((cols, width), F32)]
    else:
        out_shape = [like(wide, BF16)] * 4 + [like(cut, BF16)] * 2 + [like((rows, width), F32)]
    vmem = pltpu.VMEM
    scratch = [vmem((rows, width), F32)] * 2 + [vmem((8, rows), F32)]
    scratch += [vmem(wide, BF16)] * 6 + [vmem(cut, BF16)] * 2
    if prev:
        scratch += [vmem((prev, *wide), BF16)] * 4 + [vmem((prev, *cut), BF16)] * 2
    if last:
        scratch += [vmem((cols, width), F32)]
    else:
        scratch += [vmem((rows, width), F32)] + [vmem(wide, BF16)] * 2
        scratch += [vmem((width // 128, width, 128), BF16)] * 2 + [vmem((rows, width), F32)]
    dma = pltpu.SemaphoreType.DMA
    scratch += [dma((n_parts + 1 + n_lev,)), dma((max(n_state, 1),)), dma((n_next + 2 * n_tiles,)), dma((8,))]
    operands = [start, *parts, white, *[a for a, _, _ in levels], *[a for s in state for a in s], *following]
    operands += [base] if last else list(v_pair)
    return pl.pallas_call(
        kernel,
        out_shape=tuple(out_shape),
        in_specs=[pl.BlockSpec(memory_space=pltpu.SMEM)] + [ANY] * (len(operands) - 1),
        out_specs=tuple([ANY] * len(out_shape)),
        scratch_shapes=scratch,
        name=f"group{prev}",
        cost_estimate=pl.CostEstimate(flops=cost, bytes_accessed=1 << 20, transcendentals=0),
        compiler_params=pltpu.CompilerParams(vmem_limit_bytes=58 << 20),
    )(*operands)


def body(activations, out_grads, inverse):
    num_dev = lax.axis_size("dev")
    num_rep = lax.axis_size("rep")
    examples = activations.shape[1]
    width = KI * KO
    rows = examples * num_dev
    half = rows // 2
    features = make_features(activations, out_grads, num_dev)
    own = lax.all_to_all(features, "dev", split_axis=0, concat_axis=0, tiled=True).reshape(rows, width)
    v = inverse[0]

    up = [(i, (i + 1) % num_rep) for i in range(num_rep)]
    down = [(i, (i - 1) % num_rep) for i in range(num_rep)]
    across = [(i, (i + 2) % num_rep) for i in range(num_rep)]
    own0 = own[:half]
    below0, above0 = lax.ppermute(own0, "rep", up), lax.ppermute(own0, "rep", down)

    white, vh, vl, terms = own_white(own, v, num_dev)
    spread = lax.all_to_all(terms, "dev", split_axis=0, concat_axis=0, tiled=True)
    lev = jnp.sum(spread, axis=0) / (num_dev * width)
    lev_rows = jnp.broadcast_to(jnp.pad(lev, (0, width - rows))[None], (8, width))
    tail = jnp.concatenate([own[half:], lev_rows], axis=0)
    below1, above1 = lax.ppermute(tail, "rep", up), lax.ppermute(tail, "rep", down)

    count = width // num_rep
    start = (lax.axis_index("rep") * count).astype(jnp.int32)[None]
    step = lambda parts, w, levels, state, following, base=None: group_step(
        parts, w, levels, state, following, start, (vh, vl), base, 1 << 34
    )
    out = step([own], white, [(lev_rows, 0, rows)], [], [below0, above0])
    state, w = [out[:6]], out[6]
    below0s, above1s, w = lax.optimization_barrier((below0, above1, w))
    far0, far1 = lax.ppermute(below0s, "rep", up), lax.ppermute(above1s, "rep", down)
    out = step([below0, above0], w, [(below1, 0, half), (above1, 0, half)], state, [below1, above1])
    state, w = state + [out[:6]], out[6]
    out = step([below1, above1], w, [(below1, half, half), (above1, half, half)], state, [far0, far1])
    state, w = state + [out[:6]], out[6]
    (updated,) = step([far0, far1], w, [(far1, 0, rows)], state, [], v)

    returned = lax.all_to_all(
        white.reshape(num_dev, examples, 1, width), "dev", split_axis=0, concat_axis=2, tiled=True
    )
    whitened_out = returned.reshape(1, examples, num_dev * width)
    lev_out = lax.dynamic_slice_in_dim(lev, lax.axis_index("dev") * examples, examples, 0)[None]
    return (whitened_out, lev_out, updated.reshape(1, count, width))


def solution(mesh):
    in_specs = (P("rep", "dev", None, None), P("rep", "dev", None, None), P("dev", None, None))
    out_specs = (P("rep", "dev", None), P("rep", "dev"), P("dev", "rep", None))
    return jax.shard_map(body, mesh=mesh, in_specs=in_specs, out_specs=out_specs, check_vma=False)
```
